32 devices in a mesh: seq: 8 (over y, x, core), head: 4 (over z).
Axes of the slice: x: 2, y: 2, z: 4, core: 2. Of those that a mesh axis runs over, the one named last changes fastest.
Arguments:
- queries: bfloat16 [256, 128, 576], P('seq', 'head'), may hold values from -1024 to 1024
- latents: bfloat16 [1024, 576], P('seq'), may hold values from -6 to 6
- out_grad: bfloat16 [256, 128, 512], P('seq', 'head'), may hold values from -6 to 6
- layer_out: bfloat16 [256, 128, 512], P('seq', 'head'), may hold values from -4 to 4
- query_start: int32 [8], P('seq'), may hold values from 0 to 1023, as said below
Outputs:
- query_grad: bfloat16 [256, 128, 576], P('seq', 'head')
- latent_grad: float32 [1024, 576], P(('seq', 'head'))
The draws below stay inside these ranges and needn't reach their ends.
Inputs may be any that keep to these rules, and one draw needn't show every extreme that they name: Shard i holds the 32 queries at consecutive positions from query_start[i]; queries past the last latent position see every latent row.
All inputs are finite; a program needn't handle non-finite values.
Results may differ from the reference program's by a relative error of at most 0.0049.
Values may be sent and summed in bfloat16 or wider, within the bound.
A program may use at most 64 MiB of HBM per device.

```python
import jax
import jax.numpy as jnp
from jax import lax

HEADS = 128
DL = 512
DR = 64
Q_DEV = 32
DK = 576
QUERIES = 256
S_TOTAL = 1024
SHARDS = 8


def shared_draw(key):
    latent_key = jax.random.fold_in(key, 11)
    query_key = jax.random.fold_in(key, 12)
    latent_rows = jax.random.normal(latent_key, (S_TOTAL, DK), jnp.float32)
    query_rows = jax.random.normal(query_key, (QUERIES, HEADS, DK), jnp.float32)
    latent_rows = jnp.clip(latent_rows, -6.0, 6.0)
    query_rows = jnp.clip(query_rows, -1024.0, 1024.0)
    return (latent_rows, query_rows)


def draw_queries(key, part):
    return shared_draw(key)[1].astype(jnp.bfloat16)


def draw_latents(key, part):
    return shared_draw(key)[0].astype(jnp.bfloat16)


def draw_query_start(key, part):
    starts = jax.random.randint(jax.random.fold_in(key, 21), (SHARDS,), 0, S_TOTAL, jnp.int32)
    order = jax.random.permutation(jax.random.fold_in(key, 22), SHARDS)
    starts = starts.at[order[0]].set(0)
    starts = starts.at[order[1]].set(S_TOTAL - 1)
    return starts.astype(jnp.int32)


def shard_levels(rng, shape, pieces, smallest, top_value):
    loudness, own = 1.0, jax.random.fold_in(rng, 6)
    for position, blocks in pieces:
        draws = jnp.exp(jax.random.uniform(jax.random.fold_in(own, position), (blocks,), jnp.float32, smallest / len(pieces), top_value / len(pieces)))
        loudness = loudness * jnp.repeat(draws, shape[position] // blocks).reshape([-1 if axis == position else 1 for axis in range(len(shape))])
    return loudness


def normal_values(rng, extent, spread, reach, shards=(), held_as=jnp.bfloat16):
    result = spread * jax.random.normal(rng, extent, jnp.float32)
    if shards:
        result = result * shard_levels(rng, extent, shards, -0.22, 0.18)
    return jnp.clip(result, -reach, reach).astype(held_as)


def setup_inputs(seed: int = 0) -> dict:
    key_of = jax.random.split(jax.random.key(seed), 6)
    return {
        "queries": draw_queries(jax.random.fold_in(key_of[5], 71), 0),
        "latents": draw_latents(jax.random.fold_in(key_of[5], 71), 0),
        "out_grad": normal_values(key_of[2], (QUERIES, HEADS, DL), 1.0, 6.0, ((0, 8), (1, 4))),
        "layer_out": normal_values(key_of[3], (QUERIES, HEADS, DL), 0.5, 4.0, ((0, 8), (1, 4))),
        "query_start": draw_query_start(jax.random.fold_in(key_of[5], 71), 0),
    }


score_scale = 192 ** -0.5


def reference(queries, latents, out_grad, layer_out, query_start):
    query_pos = (query_start[:, None] + jnp.arange(Q_DEV, dtype=jnp.int32)[None, :]).reshape(-1)
    key_pos = jnp.arange(S_TOTAL, dtype=jnp.int32)
    visible = key_pos[None, :] <= query_pos[:, None]
    row_delta = jnp.sum(out_grad.astype(jnp.float32) * layer_out.astype(jnp.float32), axis=2)
    values = latents[:, :DL]

    def per_head(grad_sum, head_items):
        head_query, head_grad, head_delta = head_items
        scores = jnp.dot(head_query, latents.T, preferred_element_type=jnp.float32) * score_scale
        scores = jnp.where(visible, scores, -jnp.inf)
        top = jnp.max(scores, axis=1, keepdims=True)
        log_norm = top + jnp.log(jnp.sum(jnp.exp(scores - top), axis=1, keepdims=True))
        weights = jnp.exp(scores - log_norm)
        prob_grad = jnp.dot(head_grad, values.T, preferred_element_type=jnp.float32)
        dscore = (score_scale * weights * (prob_grad - head_delta[:, None])).astype(jnp.bfloat16)
        query_term = jnp.dot(dscore, latents, preferred_element_type=jnp.float32)
        key_term = jnp.dot(dscore.T, head_query, preferred_element_type=jnp.float32)
        value_term = jnp.dot(weights.astype(jnp.bfloat16).T, head_grad, preferred_element_type=jnp.float32)
        key_term = key_term + jnp.pad(value_term, ((0, 0), (0, DR)))
        return grad_sum + key_term, query_term.astype(jnp.bfloat16)

    start_sum = jnp.zeros((S_TOTAL, DK), jnp.float32)
    latent_grad, query_terms = lax.scan(
        per_head, start_sum,
        (jnp.moveaxis(queries, 1, 0), jnp.moveaxis(out_grad, 1, 0), row_delta.T))
    query_grad = jnp.moveaxis(query_terms, 0, 1)
    return query_grad, latent_grad
```

```python
import functools

import jax
import jax.numpy as jnp
from jax import lax
from jax.experimental import pallas as pl
from jax.experimental.pallas import tpu as pltpu
from jax.sharding import PartitionSpec as P

score_scale = 192 ** (-0.5)
masked_score = -1e30
MESH = pl.DeviceIdType.MESH
NT = (((1,), (1,)), ((), ()))
TN = (((0,), (0,)), ((), ()))


def fused_kernel(
    n_seq, n_head, head_count, tile,
    start_ref, q_hbm, lat_hbm, og_hbm, lo_hbm,
    qgrad_hbm, lgrad_ref,
    q, og, lo, keys, scores, pgrad, w16, ds, delta, run_max, run_sum,
    part, send1, rx1, send2, rx2, own, send3, rx3, qout,
    load_sem, out_sem, ag_send, ag_recv, fw_send, fw_recv,
    s1_send, s1_recv, s2_send, s2_recv, s3_send, s3_recv,
):
    f32, bf16 = jnp.float32, jnp.bfloat16
    me = lax.axis_index("seq")
    my_head = lax.axis_index("head")
    chips = n_seq // 2
    chip, core = me // 2, me % 2
    sibling = chip * 2 + 1 - core
    rows, width = q.shape
    value_width = og.shape[1]
    kb = lat_hbm.shape[0]
    tiles = rows // tile
    piece = kb // n_head

    def peer(step):
        return ((chip + step + chips) % chips) * 2 + core

    loads = [
        pltpu.make_async_copy(lat_hbm, keys.at[pl.ds(0, kb)], load_sem.at[0]),
        pltpu.make_async_copy(q_hbm, q, load_sem.at[1]),
        pltpu.make_async_copy(og_hbm, og, load_sem.at[2]),
        pltpu.make_async_copy(lo_hbm, lo, load_sem.at[3]),
    ]
    for copy in loads:
        copy.start()

    barrier = pltpu.get_barrier_semaphore()
    pl.semaphore_signal(barrier, inc=1, device_id={"seq": sibling}, device_id_type=MESH)
    for step in range(1, chips):
        pl.semaphore_signal(barrier, inc=1, device_id={"seq": peer(step)}, device_id_type=MESH)
    for step in range(1, n_head):
        pl.semaphore_signal(
            barrier, inc=1, device_id={"head": (my_head + step) % n_head}, device_id_type=MESH
        )
    pl.semaphore_wait(barrier, chips + n_head - 1)

    def slot(k, b):
        return keys.at[pl.ds((2 * k + b) * kb, kb)]

    gathers = [None] * chips
    for k in range(1, chips):
        gathers[k] = pltpu.make_async_remote_copy(
            src_ref=lat_hbm, dst_ref=slot(k, 0), send_sem=ag_send.at[k], recv_sem=ag_recv.at[k],
            device_id={"seq": peer(k)}, device_id_type=MESH,
        )
        gathers[k].start()
    relays = [
        pltpu.make_async_remote_copy(
            src_ref=lat_hbm if k == 0 else slot(k, 0), dst_ref=slot(k, 1),
            send_sem=fw_send.at[k], recv_sem=fw_recv.at[k],
            device_id={"seq": sibling}, device_id_type=MESH,
        )
        for k in range(chips)
    ]
    relays[0].start()

    loads[2].wait()
    loads[3].wait()
    ones = jnp.ones((8, value_width), bf16)
    for t in range(tiles):
        at = pl.ds(t * tile, tile)
        product = og[at, :].astype(f32) * lo[at, :].astype(f32)
        high = product.astype(bf16)
        low = (product - high.astype(f32)).astype(bf16)
        total = lax.dot_general(ones, high, NT, preferred_element_type=f32)
        total += lax.dot_general(ones, low, NT, preferred_element_type=f32)
        delta[:, at] = total[0:1, :]
    loads[0].wait()
    loads[1].wait()

    first_query = start_ref[0]
    pair = 2 * kb

    def score_pair(k):
        base = k * pair
        owner = (chip - k + chips) % chips
        row = lax.broadcasted_iota(jnp.int32, (pair, 1), 0)
        second = row // kb
        key_pos = (owner * 2 + (core + second) % 2) * kb + row % kb
        block = keys[pl.ds(base, pair), :]
        for t in range(tiles):
            at = pl.ds(t * tile, tile)
            lane = lax.broadcasted_iota(jnp.int32, (1, tile), 1) + t * tile
            query_pos = first_query + lane // head_count
            s = lax.dot_general(block, q[at, :], NT, preferred_element_type=f32) * score_scale
            s = jnp.where(key_pos <= query_pos, s, masked_score)
            scores[pl.ds(base, pair), at] = s
            top = jnp.max(s, axis=0, keepdims=True)
            if k == 0:
                run_max[:, at] = top
                run_sum[:, at] = jnp.sum(jnp.exp(s - top), axis=0, keepdims=True)
            else:
                before = run_max[:, at]
                top = jnp.maximum(before, top)
                run_max[:, at] = top
                run_sum[:, at] = run_sum[:, at] * jnp.exp(before - top) + jnp.sum(
                    jnp.exp(s - top), axis=0, keepdims=True
                )
            pgrad[pl.ds(base, pair), at] = lax.dot_general(
                block[:, :value_width], og[at, :], NT, preferred_element_type=f32
            )

    for k in range(1, chips):
        gathers[k].wait_recv()
        relays[k].start()
        relays[k - 1].wait_recv()
        score_pair(k - 1)
    relays[chips - 1].wait_recv()
    score_pair(chips - 1)

    run_max[...] = run_max[...] + jnp.log(run_sum[...])

    def grad_pair(k):
        base = k * pair
        for t in range(tiles):
            at = pl.ds(t * tile, tile)
            w = jnp.exp(scores[pl.ds(base, pair), at] - run_max[:, at])
            w16[:, at] = w.astype(bf16)
            ds[pl.ds(base, pair), at] = (
                score_scale * w * (pgrad[pl.ds(base, pair), at] - delta[:, at])
            ).astype(bf16)
        term = jnp.dot(ds[pl.ds(base, pair), :], q[...], preferred_element_type=f32)
        value = jnp.dot(w16[...], og[...], preferred_element_type=f32)
        wide = term[:, :value_width] + value
        tail = term[:, value_width:]
        part[k, :, :value_width] = wide[:kb]
        part[k, :, value_width:] = tail[:kb]
        send1[k, :, :value_width] = wide[kb:].astype(bf16)
        send1[k, :, value_width:] = tail[kb:].astype(bf16)

    pair_sends = [
        pltpu.make_async_remote_copy(
            src_ref=send1.at[k], dst_ref=rx1.at[k], send_sem=s1_send.at[k], recv_sem=s1_recv.at[k],
            device_id={"seq": sibling}, device_id_type=MESH,
        )
        for k in range(chips)
    ]
    chip_sends = [None] + [
        pltpu.make_async_remote_copy(
            src_ref=send2.at[k], dst_ref=rx2.at[k], send_sem=s2_send.at[k], recv_sem=s2_recv.at[k],
            device_id={"seq": peer(-k)}, device_id_type=MESH,
        )
        for k in range(1, chips)
    ]

    def forward(k):
        pair_sends[k].wait_recv()
        send2[k] = (part[k] + rx1[k].astype(f32)).astype(bf16)
        chip_sends[k].start()

    order = list(range(1, chips)) + [0]
    lag = 2
    for n, k in enumerate(order):
        grad_pair(k)
        pair_sends[k].start()
        if n >= lag and order[n - lag] != 0:
            forward(order[n - lag])
    for n in range(max(0, len(order) - lag), len(order)):
        if order[n] != 0:
            forward(order[n])

    for t in range(tiles):
        at = pl.ds(t * tile, tile)
        qout[at, :] = lax.dot_general(
            ds[:, at], keys[...], TN, preferred_element_type=f32
        ).astype(bf16)
    store = pltpu.make_async_copy(qout, qgrad_hbm, out_sem)
    store.start()

    pair_sends[0].wait_recv()
    total = part[0] + rx1[0].astype(f32)
    for k in range(1, chips):
        chip_sends[k].wait_recv()
        total = total + rx2[k].astype(f32)
    for h in range(n_head):
        own[h] = total[h * piece : (h + 1) * piece]
        send3[h] = total[h * piece : (h + 1) * piece].astype(bf16)
    head_sends = [None] * n_head
    for k in range(1, n_head):
        target = (my_head + k) % n_head
        head_sends[k] = pltpu.make_async_remote_copy(
            src_ref=send3.at[target], dst_ref=rx3.at[k],
            send_sem=s3_send.at[k], recv_sem=s3_recv.at[k],
            device_id={"head": target}, device_id_type=MESH,
        )
        head_sends[k].start()
    result = own[my_head]
    for k in range(1, n_head):
        head_sends[k].wait_recv()
        result = result + rx3[k].astype(f32)
    lgrad_ref[...] = result

    for k in range(1, n_head):
        head_sends[k].wait_send()
    for k in range(1, chips):
        gathers[k].wait_send()
        chip_sends[k].wait_send()
    for k in range(chips):
        relays[k].wait_send()
        pair_sends[k].wait_send()
    store.wait()


def per_device(n_seq, n_head, queries, latents, out_grad, layer_out, query_start):
    query_count, head_count, width = queries.shape
    value_width = out_grad.shape[2]
    rows = query_count * head_count
    kb = latents.shape[0]
    total_keys = kb * n_seq
    chips = n_seq // 2
    piece = kb // n_head
    tile = min(256, rows)
    f32, bf16 = jnp.float32, jnp.bfloat16
    anywhere = pl.BlockSpec(memory_space=pl.ANY)
    dma = pltpu.SemaphoreType.DMA
    query_grad, latent_grad = pl.pallas_call(
        functools.partial(fused_kernel, n_seq, n_head, head_count, tile),
        out_shape=(
            jax.ShapeDtypeStruct((rows, width), bf16),
            jax.ShapeDtypeStruct((piece, width), f32),
        ),
        in_specs=[pl.BlockSpec(memory_space=pltpu.SMEM)] + [anywhere] * 4,
        out_specs=(anywhere, pl.BlockSpec(memory_space=pltpu.VMEM)),
        scratch_shapes=[
            pltpu.VMEM((rows, width), bf16),
            pltpu.VMEM((rows, value_width), bf16),
            pltpu.VMEM((rows, value_width), bf16),
            pltpu.VMEM((total_keys, width), bf16),
            pltpu.VMEM((total_keys, rows), f32),
            pltpu.VMEM((total_keys, rows), f32),
            pltpu.VMEM((2 * kb, rows), bf16),
            pltpu.VMEM((total_keys, rows), bf16),
            pltpu.VMEM((1, rows), f32),
            pltpu.VMEM((1, rows), f32),
            pltpu.VMEM((1, rows), f32),
            pltpu.VMEM((chips, kb, width), f32),
            pltpu.VMEM((chips, kb, width), bf16),
            pltpu.VMEM((chips, kb, width), bf16),
            pltpu.VMEM((chips, kb, width), bf16),
            pltpu.VMEM((chips, kb, width), bf16),
            pltpu.VMEM((n_head, piece, width), f32),
            pltpu.VMEM((n_head, piece, width), bf16),
            pltpu.VMEM((n_head, piece, width), bf16),
            pltpu.VMEM((rows, width), bf16),
            dma((4,)), dma(()),
            dma((chips,)), dma((chips,)), dma((chips,)), dma((chips,)),
            dma((chips,)), dma((chips,)), dma((chips,)), dma((chips,)),
            dma((n_head,)), dma((n_head,)),
        ],
        compiler_params=pltpu.CompilerParams(
            collective_id=0, has_side_effects=True, vmem_limit_bytes=56 * 1024 * 1024
        ),
    )(
        query_start,
        queries.reshape(rows, width),
        latents,
        out_grad.reshape(rows, value_width),
        layer_out.reshape(rows, value_width),
    )
    return query_grad.reshape(query_count, head_count, width), latent_grad


def solution(mesh):
    placed = (
        P("seq", "head", None),
        P("seq", None),
        P("seq", "head", None),
        P("seq", "head", None),
        P("seq"),
    )
    return jax.shard_map(
        functools.partial(per_device, mesh.shape["seq"], mesh.shape["head"]),
        mesh=mesh,
        in_specs=placed,
        out_specs=(P("seq", "head", None), P(("seq", "head"), None)),
        check_vma=False,
    )
```

```python
import functools

import jax
import jax.numpy as jnp
from jax import lax
from jax.experimental import pallas as pl
from jax.experimental.pallas import tpu as pltpu
from jax.sharding import PartitionSpec as P

score_scale = 192 ** (-0.5)
masked_score = -1e30
MESH = pl.DeviceIdType.MESH
NT = (((1,), (1,)), ((), ()))
TN = (((0,), (0,)), ((), ()))


def fused_kernel(
    n_seq, n_head, head_count, tile, cut,
    start_ref, q_hbm, lat_hbm, og_hbm, lo_hbm,
    qout, lgrad_ref,
    q, og, lo, keys_t, keys, scores, pgrad, w16, ds, delta, run_max, run_sum,
    part, send1, rx1, send2, rx2, own, send3, rx3, own4, send4, rx4, send5, rx5,
    load_sem, ag_send, ag_recv, fw_send, fw_recv,
    s1_send, s1_recv, s2_send, s2_recv, s3_send, s3_recv,
    s4_send, s4_recv, s5_send, s5_recv,
):
    f32, bf16 = jnp.float32, jnp.bfloat16
    me = lax.axis_index("seq")
    my_head = lax.axis_index("head")
    chips = n_seq // 2
    chip, core = me // 2, me % 2
    sibling = chip * 2 + 1 - core
    rows, width = q.shape
    value_width = og.shape[1]
    kb = lat_hbm.shape[1]
    tiles = rows // tile
    piece = kb // n_head

    def other_chip(k):
        found = 0
        for bit in range(chips.bit_length() - 1):
            size = 2**bit
            found += (chip // size % 2 + k // size % 2) % 2 * size
        return found

    def peer(k):
        return other_chip(k) * 2 + core

    loads = [
        pltpu.make_async_copy(lat_hbm, keys_t.at[0], load_sem.at[0]),
        pltpu.make_async_copy(q_hbm, q, load_sem.at[1]),
        pltpu.make_async_copy(og_hbm, og, load_sem.at[2]),
        pltpu.make_async_copy(lo_hbm, lo, load_sem.at[3]),
    ]
    for copy in loads:
        copy.start()

    barrier = pltpu.get_barrier_semaphore()
    pl.semaphore_signal(barrier, inc=1, device_id={"seq": sibling}, device_id_type=MESH)
    for step in range(1, chips):
        pl.semaphore_signal(barrier, inc=1, device_id={"seq": peer(step)}, device_id_type=MESH)
    for step in range(1, n_head):
        pl.semaphore_signal(
            barrier, inc=1, device_id={"head": (my_head + step) % n_head}, device_id_type=MESH
        )
    pl.semaphore_wait(barrier, chips + n_head - 1)

    def slot(k, b):
        return keys_t.at[2 * k + b]

    side = my_head % 2
    partner = my_head + 1 - 2 * side
    quarter = width // 4
    outer = pl.ds(pl.multiple_of(side * 3 * quarter, quarter), quarter)
    middle = pl.ds(quarter, 2 * quarter)

    def gather(k, part_rows, index):
        return pltpu.make_async_remote_copy(
            src_ref=lat_hbm.at[part_rows, :], dst_ref=keys_t.at[2 * k, part_rows, :],
            send_sem=ag_send.at[k, index], recv_sem=ag_recv.at[k, index],
            device_id={"seq": peer(k)}, device_id_type=MESH,
        )

    outer_gathers = [None] + [gather(k, outer, 0) for k in range(1, chips)]
    middle_gathers = [None] + [gather(k, middle, 1) for k in range(1, chips)]
    swaps = [None] + [
        pltpu.make_async_remote_copy(
            src_ref=keys_t.at[2 * k, outer, :], dst_ref=keys_t.at[2 * k, outer, :],
            send_sem=ag_send.at[k, 2], recv_sem=ag_recv.at[k, 2],
            device_id={"head": partner}, device_id_type=MESH,
        )
        for k in range(1, chips)
    ]
    for k in range(1, chips):
        outer_gathers[k].start()
    for k in range(1, chips):
        middle_gathers[k].start()
    relays = [
        pltpu.make_async_remote_copy(
            src_ref=lat_hbm if k == 0 else slot(k, 0), dst_ref=slot(k, 1),
            send_sem=fw_send.at[k], recv_sem=fw_recv.at[k],
            device_id={"seq": sibling}, device_id_type=MESH,
        )
        for k in range(chips)
    ]
    relays[0].start()

    loads[2].wait()
    loads[3].wait()
    ones = jnp.ones((8, value_width), bf16)
    for t in range(tiles):
        at = pl.ds(t * tile, tile)
        product = og[at, :].astype(f32) * lo[at, :].astype(f32)
        high = product.astype(bf16)
        low = (product - high.astype(f32)).astype(bf16)
        total = lax.dot_general(ones, high, NT, preferred_element_type=f32)
        total += lax.dot_general(ones, low, NT, preferred_element_type=f32)
        delta[:, at] = total[0:1, :]
    for k in range(1, chips):
        outer_gathers[k].wait_recv()
        swaps[k].start()
    loads[0].wait()
    loads[1].wait()

    first_query = start_ref[0]
    pair = 2 * kb

    def score_pair(k):
        base = k * pair
        owner = other_chip(k)
        row = lax.broadcasted_iota(jnp.int32, (pair, 1), 0)
        second = row // kb
        key_pos = (owner * 2 + (core + second) % 2) * kb + row % kb
        for b in range(2):
            keys[pl.ds(base + b * kb, kb), :] = keys_t[2 * k + b].T
        block = keys[pl.ds(base, pair), :]
        for t in range(tiles):
            at = pl.ds(t * tile, tile)
            lane = lax.broadcasted_iota(jnp.int32, (1, tile), 1) + t * tile
            query_pos = first_query + lane // head_count
            s = lax.dot_general(block, q[at, :], NT, preferred_element_type=f32) * score_scale
            s = jnp.where(key_pos <= query_pos, s, masked_score)
            scores[pl.ds(base, pair), at] = s
            top = jnp.max(s, axis=0, keepdims=True)
            if k == 0:
                run_max[:, at] = top
                run_sum[:, at] = jnp.sum(jnp.exp(s - top), axis=0, keepdims=True)
            else:
                before = run_max[:, at]
                top = jnp.maximum(before, top)
                run_max[:, at] = top
                run_sum[:, at] = run_sum[:, at] * jnp.exp(before - top) + jnp.sum(
                    jnp.exp(s - top), axis=0, keepdims=True
                )
            pgrad[pl.ds(base, pair), at] = lax.dot_general(
                block[:, :value_width], og[at, :], NT, preferred_element_type=f32
            )

    def arrived(k):
        middle_gathers[k].wait_recv()
        swaps[k].wait_recv()
        relays[k].start()

    relays[0].wait_recv()
    score_pair(0)
    arrived(1)
    for k in range(2, chips):
        arrived(k)
        relays[k - 1].wait_recv()
        score_pair(k - 1)
    relays[chips - 1].wait_recv()
    score_pair(chips - 1)

    run_max[...] = run_max[...] + jnp.log(run_sum[...])

    def grad_pair(k):
        base = k * pair
        for t in range(tiles):
            at = pl.ds(t * tile, tile)
            w = jnp.exp(scores[pl.ds(base, pair), at] - run_max[:, at])
            w16[:, at] = w.astype(bf16)
            ds[pl.ds(base, pair), at] = (
                score_scale * w * (pgrad[pl.ds(base, pair), at] - delta[:, at])
            ).astype(bf16)
        term = jnp.dot(ds[pl.ds(base, pair), :], q[...], preferred_element_type=f32)
        value = jnp.dot(w16[...], og[...], preferred_element_type=f32)
        wide = term[:, :value_width] + value
        tail = term[:, value_width:]
        part[k, :, :value_width] = wide[:kb]
        part[k, :, value_width:] = tail[:kb]
        send1[k, :, :value_width] = wide[kb:].astype(bf16)
        send1[k, :, value_width:] = tail[kb:].astype(bf16)

    def pack(wide):
        body = wide[:, : value_width - cut]
        tail = wide[:, value_width - cut :]
        half = piece // 2
        lanes = jnp.concatenate([tail[:half], tail[half:]], axis=1)
        return jnp.concatenate([body, lanes], axis=0)

    def chip_copy(src, dst, send_sem, recv_sem, k):
        return pltpu.make_async_remote_copy(
            src_ref=src.at[k], dst_ref=dst.at[k], send_sem=send_sem.at[k], recv_sem=recv_sem.at[k],
            device_id={"seq": peer(k)}, device_id_type=MESH,
        )

    pair_sends = [
        pltpu.make_async_remote_copy(
            src_ref=send1.at[k], dst_ref=rx1.at[k], send_sem=s1_send.at[k], recv_sem=s1_recv.at[k],
            device_id={"seq": sibling}, device_id_type=MESH,
        )
        for k in range(chips)
    ]
    chip_sends = [None] + [
        chip_copy(send2, rx2, s2_send, s2_recv, k) for k in range(1, chips)
    ]
    late_chip_sends = [None] + [
        chip_copy(send5, rx5, s5_send, s5_recv, k) for k in range(1, chips)
    ]
    early_head_sends = [[None] * n_head for _ in range(chips)]
    for k in range(chips):
        for d in range(1, n_head):
            target = (my_head + d) % n_head
            early_head_sends[k][d] = pltpu.make_async_remote_copy(
                src_ref=send4.at[k, target], dst_ref=rx4.at[k, d],
                send_sem=s4_send.at[k, d], recv_sem=s4_recv.at[k, d],
                device_id={"head": target}, device_id_type=MESH,
            )

    def forward(k):
        pair_sends[k].wait_recv()
        total = part[k] + rx1[k].astype(f32)
        if k:
            send2[k] = total[:, :cut].astype(bf16)
            chip_sends[k].start()
        else:
            part[0, :, :cut] = total[:, :cut]
        for h in range(n_head):
            packed = pack(total[h * piece : (h + 1) * piece, cut:])
            own4[k, h] = packed
            send4[k, h] = packed.astype(bf16)
        for d in range(1, n_head):
            early_head_sends[k][d].start()

    def query_tile(t):
        at = pl.ds(t * tile, tile)
        qout[at, :] = lax.dot_general(
            ds[:, at], keys[...], TN, preferred_element_type=f32
        ).astype(bf16)

    order = list(range(chips - 1, -1, -1))
    lag = 1
    for n, k in enumerate(order):
        grad_pair(k)
        pair_sends[k].start()
        if n >= lag:
            forward(order[n - lag])
    for n in range(max(0, len(order) - lag), len(order)):
        forward(order[n])

    before = (tiles + 1) // 2
    for t in range(before):
        query_tile(t)

    late = None
    for k in order:
        total = own4[k, my_head]
        for d in range(1, n_head):
            early_head_sends[k][d].wait_recv()
            total = total + rx4[k, d].astype(f32)
        if k:
            send5[k] = total.astype(bf16)
            late_chip_sends[k].start()
        else:
            late = total

    total = part[0, :, :cut]
    for k in range(1, chips):
        chip_sends[k].wait_recv()
        total = total + rx2[k].astype(f32)
    for h in range(n_head):
        own[h] = total[h * piece : (h + 1) * piece]
        send3[h] = total[h * piece : (h + 1) * piece].astype(bf16)
    head_sends = [None] * n_head
    for d in range(1, n_head):
        target = (my_head + d) % n_head
        head_sends[d] = pltpu.make_async_remote_copy(
            src_ref=send3.at[target], dst_ref=rx3.at[d],
            send_sem=s3_send.at[d], recv_sem=s3_recv.at[d],
            device_id={"head": target}, device_id_type=MESH,
        )
        head_sends[d].start()

    for t in range(before, tiles):
        query_tile(t)

    for k in range(1, chips):
        late_chip_sends[k].wait_recv()
        late = late + rx5[k].astype(f32)
    half = piece // 2
    lgrad_ref[:, cut:value_width] = late[:piece]
    lgrad_ref[:half, value_width:] = late[piece:, : width - value_width]
    lgrad_ref[half:, value_width:] = late[piece:, width - value_width :]

    result = own[my_head]
    for d in range(1, n_head):
        head_sends[d].wait_recv()
        result = result + rx3[d].astype(f32)
    lgrad_ref[:, :cut] = result

    for d in range(1, n_head):
        head_sends[d].wait_send()
    for k in range(1, chips):
        outer_gathers[k].wait_send()
        middle_gathers[k].wait_send()
        swaps[k].wait_send()
        chip_sends[k].wait_send()
        late_chip_sends[k].wait_send()
    for k in range(chips):
        relays[k].wait_send()
        pair_sends[k].wait_send()
        for d in range(1, n_head):
            early_head_sends[k][d].wait_send()


def per_device(n_seq, n_head, queries, latents, out_grad, layer_out, query_start):
    query_count, head_count, width = queries.shape
    value_width = out_grad.shape[2]
    rows = query_count * head_count
    kb = latents.shape[0]
    total_keys = kb * n_seq
    chips = n_seq // 2
    piece = kb // n_head
    tile = min(256, rows)
    cut = value_width - 128
    packed = piece + piece * (width - value_width) // 128
    f32, bf16 = jnp.float32, jnp.bfloat16
    anywhere = pl.BlockSpec(memory_space=pl.ANY)
    dma = pltpu.SemaphoreType.DMA
    query_grad, latent_grad = pl.pallas_call(
        functools.partial(fused_kernel, n_seq, n_head, head_count, tile, cut),
        out_shape=(
            pltpu.VMEM((rows, width), bf16),
            pltpu.VMEM((piece, width), f32),
        ),
        in_specs=[pl.BlockSpec(memory_space=pltpu.SMEM)] + [anywhere] * 4,
        out_specs=(pl.BlockSpec(memory_space=pltpu.VMEM),) * 2,
        scratch_shapes=[
            pltpu.VMEM((rows, width), bf16),
            pltpu.VMEM((rows, value_width), bf16),
            pltpu.VMEM((rows, value_width), bf16),
            pltpu.VMEM((2 * chips, width, kb), bf16),
            pltpu.VMEM((total_keys, width), bf16),
            pltpu.VMEM((total_keys, rows), f32),
            pltpu.VMEM((total_keys, rows), f32),
            pltpu.VMEM((2 * kb, rows), bf16),
            pltpu.VMEM((total_keys, rows), bf16),
            pltpu.VMEM((1, rows), f32),
            pltpu.VMEM((1, rows), f32),
            pltpu.VMEM((1, rows), f32),
            pltpu.VMEM((chips, kb, width), f32),
            pltpu.VMEM((chips, kb, width), bf16),
            pltpu.VMEM((chips, kb, width), bf16),
            pltpu.VMEM((chips, kb, cut), bf16),
            pltpu.VMEM((chips, kb, cut), bf16),
            pltpu.VMEM((n_head, piece, cut), f32),
            pltpu.VMEM((n_head, piece, cut), bf16),
            pltpu.VMEM((n_head, piece, cut), bf16),
            pltpu.VMEM((chips, n_head, packed, 128), f32),
            pltpu.VMEM((chips, n_head, packed, 128), bf16),
            pltpu.VMEM((chips, n_head, packed, 128), bf16),
            pltpu.VMEM((chips, packed, 128), bf16),
            pltpu.VMEM((chips, packed, 128), bf16),
            dma((4,)),
            dma((chips, 3)), dma((chips, 3)), dma((chips,)), dma((chips,)),
            dma((chips,)), dma((chips,)), dma((chips,)), dma((chips,)),
            dma((n_head,)), dma((n_head,)),
            dma((chips, n_head)), dma((chips, n_head)), dma((chips,)), dma((chips,)),
        ],
        compiler_params=pltpu.CompilerParams(
            collective_id=0, has_side_effects=True, vmem_limit_bytes=56 * 1024 * 1024
        ),
    )(
        query_start,
        queries.reshape(rows, width),
        latents.T,
        out_grad.reshape(rows, value_width),
        layer_out.reshape(rows, value_width),
    )
    return query_grad.reshape(query_count, head_count, width), latent_grad


def solution(mesh):
    placed = (
        P("seq", "head", None),
        P("seq", None),
        P("seq", "head", None),
        P("seq", "head", None),
        P("seq"),
    )
    return jax.shard_map(
        functools.partial(per_device, mesh.shape["seq"], mesh.shape["head"]),
        mesh=mesh,
        in_specs=placed,
        out_specs=(P("seq", "head", None), P(("seq", "head"), None)),
        check_vma=False,
    )
```
